32 devices in a mesh: wide: 8 (over z, x), narrow: 4 (over y, core).
Axes of the slice: x: 2, y: 2, z: 4, core: 2. Of those that a mesh axis runs over, the one named last changes fastest.
Arguments:
- tiles: bfloat16 [4, 64, 2048, 128], P(None, None, ('wide', 'narrow')), may hold values from -4 to 4
- slot: int32 [32, 4], P(('wide', 'narrow')), may hold values from 0 to 3, each once within a row
- a_factor: float32 [2048, 256], P(('wide', 'narrow')), may hold values from -1.6 to 1.6
- b_factor: float32 [1024, 256], P('wide'), may hold values from -1.6 to 1.6
- c_factor: float32 [512, 256], P('wide'), may hold values from -1.6 to 1.6
- a_velocity: float32 [2048, 256], P(('wide', 'narrow')), may hold values from -0.012 to 0.012
- b_velocity: float32 [1024, 256], P('wide'), may hold values from -0.012 to 0.012
- c_velocity: float32 [512, 256], P('wide'), may hold values from -0.012 to 0.012
Outputs:
- a_out: float32 [2048, 256], P(('wide', 'narrow'))
- b_out: float32 [1024, 256], P('wide')
- c_out: float32 [512, 256], P('wide')
The draws below stay inside these ranges and needn't reach their ends.
Inputs may be any that keep to these rules, and one draw needn't show every extreme that they name: Each row of slot names every one of the 4 tiles of its row block once.
All inputs are finite; a program needn't handle non-finite values.
Results may differ from the reference program's by a relative error of at most 0.0003.
Values sent between devices are 32-bit elements; how exact they have to be, the bound alone decides.
No kernel may reach another device: no remote copies, remote signals or barrier semaphores. Data moves between devices by JAX's collectives and lax.ppermute only.
A program may use at most 64 MiB of HBM per device.

```python
import jax
import jax.numpy as jnp
from jax import lax

RANK = 256
IB = 64
JB = 128
KB = 64
STRATA = 4
SECOND_STRIDE = 1
THIRD_STRIDE = 3
G = 32
NI = 2048
NJ = 1024
NK = 512
N_WIDE = 8
N_NARROW = 4


def bounded_field(key, marker, shape, deviation):
    key = jax.random.fold_in(key, marker)
    return deviation * jax.random.truncated_normal(key, -4.0, 4.0, shape, jnp.float32)


def draw_tiles(key, part):
    return bounded_field(key, 11, (STRATA, KB, NI, JB), 1.0).astype(jnp.bfloat16)


def draw_a_factor(key, part):
    return bounded_field(key, 23, (NI, RANK), 0.4)


def draw_b_factor(key, part):
    return bounded_field(key, 37, (NJ, RANK), 0.4)


def draw_c_factor(key, part):
    return bounded_field(key, 41, (NK, RANK), 0.4)


def draw_a_velocity(key, part):
    return bounded_field(key, 53, (NI, RANK), 0.003)


def draw_b_velocity(key, part):
    return bounded_field(key, 67, (NJ, RANK), 0.003)


def draw_c_velocity(key, part):
    return bounded_field(key, 79, (NK, RANK), 0.003)


def setup_inputs(seed: int = 0) -> dict:
    streams_of = jax.random.split(jax.random.key(seed), 9)
    return {
        "tiles": draw_tiles(jax.random.fold_in(streams_of[8], 71), 0),
        "slot": jax.vmap(lambda own: jax.random.permutation(own, STRATA))(jax.random.split(streams_of[1], G)).reshape((G, STRATA)).astype(jnp.int32),
        "a_factor": draw_a_factor(jax.random.fold_in(streams_of[8], 71), 0),
        "b_factor": draw_b_factor(jax.random.fold_in(streams_of[8], 71), 0),
        "c_factor": draw_c_factor(jax.random.fold_in(streams_of[8], 71), 0),
        "a_velocity": draw_a_velocity(jax.random.fold_in(streams_of[8], 71), 0),
        "b_velocity": draw_b_velocity(jax.random.fold_in(streams_of[8], 71), 0),
        "c_velocity": draw_c_velocity(jax.random.fold_in(streams_of[8], 71), 0),
    }


momentum = 0.9
step_rate = 20.0


def tile_terms(tile, a_rows, b_rows, c_rows):
    kb, ib, jb = tile.shape
    rank = a_rows.shape[1]
    prod = (a_rows[:, None, :] * b_rows[None, :, :]).reshape(ib * jb, rank)
    recon = lax.dot_general(c_rows, prod, (((1,), (1,)), ((), ())), precision=lax.Precision.HIGHEST, preferred_element_type=jnp.float32)
    error = recon - tile.astype(jnp.float32).reshape(kb, ib * jb)
    mixed = lax.dot_general(error, c_rows, (((0,), (0,)), ((), ())), precision=lax.Precision.HIGHEST, preferred_element_type=jnp.float32)
    mixed = mixed.reshape(ib, jb, rank)
    grad_a = jnp.sum(mixed * b_rows[None, :, :], axis=1)
    part_b = jnp.sum(mixed * a_rows[:, None, :], axis=0)
    part_c = jnp.dot(error, prod, precision=lax.Precision.HIGHEST, preferred_element_type=jnp.float32)
    return grad_a, part_b, part_c


def reference(tiles, slot, a_factor, b_factor, c_factor, a_velocity, b_velocity, c_velocity):
    wide = N_WIDE
    groups = N_NARROW
    stack = tiles.reshape(STRATA, KB, wide, groups, IB, JB).transpose(2, 3, 0, 1, 4, 5)
    order = slot.reshape(wide, groups, STRATA)
    a_rows = a_factor.reshape(wide, groups, IB, RANK)
    a_vel = a_velocity.reshape(wide, groups, IB, RANK)
    b_rows = b_factor.reshape(wide, JB, RANK)
    b_vel = b_velocity.reshape(wide, JB, RANK)
    c_rows = c_factor.reshape(wide, KB, RANK)
    c_vel = c_velocity.reshape(wide, KB, RANK)
    for stratum in range(STRATA):
        def one_wide(items):
            tiles_w, order_w, a_w, b_w, c_w = items

            def one_row(tiles_n, index, a_n):
                tile = lax.dynamic_index_in_dim(tiles_n, index, 0, keepdims=False)
                return tile_terms(tile, a_n, b_w, c_w)

            return jax.vmap(one_row)(tiles_w, order_w[:, stratum], a_w)

        grad_a, part_b, part_c = lax.map(one_wide, (stack, order, a_rows, b_rows, c_rows))
        grad_b = jnp.sum(part_b, axis=1)
        grad_c = jnp.sum(part_c, axis=1)
        a_vel = momentum * a_vel + grad_a * (1.0 / (JB * KB))
        a_rows = a_rows - step_rate * a_vel
        b_vel = momentum * b_vel + grad_b * (1.0 / (groups * IB * KB))
        b_rows = b_rows - step_rate * b_vel
        c_vel = momentum * c_vel + grad_c * (1.0 / (groups * IB * JB))
        c_rows = c_rows - step_rate * c_vel
        if stratum + 1 < STRATA:
            b_rows = jnp.roll(b_rows, SECOND_STRIDE, axis=0)
            b_vel = jnp.roll(b_vel, SECOND_STRIDE, axis=0)
            c_rows = jnp.roll(c_rows, THIRD_STRIDE, axis=0)
            c_vel = jnp.roll(c_vel, THIRD_STRIDE, axis=0)
    return (a_rows.reshape(NI, RANK), b_rows.reshape(NJ, RANK), c_rows.reshape(NK, RANK))
```

```python
import functools

import jax
import jax.numpy as jnp
from jax import lax
from jax.experimental import pallas as pl
from jax.experimental.pallas import tpu as pltpu
from jax.sharding import PartitionSpec as P

STRATA = 4
SECOND_STRIDE = 1
THIRD_STRIDE = 3
CORES = 2

momentum = 0.9
step_rate = 20.0

BOTH = ("wide", "narrow")


def halves(x):
    hi = x.astype(jnp.bfloat16)
    lo = (x - hi.astype(jnp.float32)).astype(jnp.bfloat16)
    return hi, lo


def product(x, y, dims):
    xh, xl = halves(x)
    yh, yl = halves(y)
    dot = functools.partial(
        lax.dot_general, dimension_numbers=(dims, ((), ())), preferred_element_type=jnp.float32
    )
    return dot(xh, yh) + (dot(xh, yl) + dot(xl, yh))


def gram(x):
    return product(x, x, ((0,), (0,)))


def apply(x, g):
    return product(x, g, ((1,), (0,)))


def advance_a(tile, a, va, b, c, scale):
    kb, ib, jb = tile.shape
    rank = a.shape[-1]
    stacked = jnp.concatenate(halves(b[...]), axis=0)
    step = 8

    def body(n, acc):
        x = tile[pl.ds(n * step, step)].reshape(step * ib, jb)
        y = jnp.dot(
            jnp.concatenate([x, x], axis=1), stacked, preferred_element_type=jnp.float32
        ).reshape(step, ib, rank)
        cs = c[pl.ds(pl.multiple_of(n * step, step), step), :]
        for m in range(step):
            acc = acc + y[m] * cs[m : m + 1]
        return acc

    seen = lax.fori_loop(0, kb // step, body, jnp.zeros((ib, rank), jnp.float32))
    grad = apply(a[...], gram(b[...]) * gram(c[...])) - seen
    va_new = momentum * va[...] + grad * scale
    return a[...] - step_rate * va_new, va_new


def spread(tile, a, z):
    kb, ib, jb = tile.shape
    stacked = jnp.concatenate(halves(a), axis=0)

    def body(k, carry):
        x = tile[k]
        z[k] = lax.dot_general(
            jnp.concatenate([x, x], axis=0),
            stacked,
            (((0,), (0,)), ((), ())),
            preferred_element_type=jnp.float32,
        )
        return carry

    lax.fori_loop(0, kb, body, 0, unroll=4)


def first_kernel(slot, tile, a, z):
    spread(tile.at[0], a[...], z)


def window_kernel(slot, old, new, a, va, b, c, a_out, va_out, z, *, scale):
    a_new, va_new = advance_a(old.at[0], a, va, b, c, scale)
    a_out[...] = a_new
    va_out[...] = va_new
    spread(new.at[0], a_new, z)


def last_kernel(slot, old, a, va, b, c, a_out, *, scale):
    a_new, _ = advance_a(old.at[0], a, va, b, c, scale)
    a_out[...] = a_new


def gradient_kernel(core, z, a, mine, other, before, b_out, c_out, send, keep, mb, mc, *, mult_b, mult_c, parts):
    kb, jb, rank = z.shape
    first = core[0] == 0

    @pl.when(first)
    def _():
        b_out[...] = mine[0:jb]
        c_out[...] = other[0:kb]

    @pl.when(jnp.logical_not(first))
    def _():
        b_out[...] = other[0:jb]
        c_out[...] = mine[0:kb]

    step = 8

    def body(n, acc):
        at = pl.multiple_of(n * step, step)
        cs = c_out[pl.ds(at, step), :]
        rows = []
        for m in range(step):
            zk = z[at + m]
            acc = acc + zk * cs[m : m + 1]
            rows.append(jnp.sum(zk * b_out[...], axis=0, keepdims=True))
        mc[pl.ds(at, step), :] = jnp.concatenate(rows, axis=0)
        return acc

    mb[...] = lax.fori_loop(0, kb // step, body, jnp.zeros((jb, rank), jnp.float32))
    b, c = b_out[...], c_out[...]
    ata = gram(a[...])
    for_b = mult_b * (mb[...] - apply(b, ata * gram(c)))
    for_c = mult_c * (mc[...] - apply(c, ata * gram(b)))
    base = ((1.0 + momentum) * mine[...] - momentum * before[...]) * (1.0 / parts)
    keep[...] = base
    send[...] = jnp.zeros(send.shape, jnp.float32)

    @pl.when(first)
    def _():
        keep[0:jb] += for_b
        send[0:kb] = for_c

    @pl.when(jnp.logical_not(first))
    def _():
        keep[0:kb] += for_c
        send[0:jb] = for_b


def f32(*shape):
    return jax.ShapeDtypeStruct(shape, jnp.float32)


def in_vmem(n):
    return [pl.BlockSpec(memory_space=pltpu.VMEM)] * n


def shards(tiles, slot, a, b, c, va, vb, vc):
    wide = lax.axis_size("wide")
    narrow = lax.axis_size("narrow")
    parts = narrow // CORES
    core = lax.axis_index("narrow") % CORES
    _, kb, ib, jb = tiles.shape
    rank = a.shape[1]
    rows = max(jb, kb)
    scale_a = 1.0 / (jb * kb)
    mult_b = step_rate / (narrow * ib * kb)
    mult_c = step_rate / (narrow * ib * jb)
    order = slot.reshape(-1)
    core_arg = core.astype(jnp.int32).reshape(1)

    def route(where):
        return [
            (w * narrow + n, (t % wide) * narrow + u)
            for w in range(wide)
            for n in range(narrow)
            for t, u in [where(w, n)]
        ]

    def swap(x):
        return lax.ppermute(x, BOTH, route(lambda w, n: (w, n // CORES * CORES + (n + 1) % CORES)))

    def onward(x, turn):
        def where(w, n):
            stride = SECOND_STRIDE if n % CORES == 0 else THIRD_STRIDE
            return w + stride, (n + turn * CORES) % narrow

        return lax.ppermute(x, BOTH, route(where))

    def around(x, turn):
        return lax.ppermute(x, BOTH, route(lambda w, n: (w, (n + turn * CORES) % narrow)))

    def tile_spec(s):
        return pl.BlockSpec((1, kb, ib, jb), lambda i, o: (o[s], 0, 0, 0))

    def over_tiles(kernel, strata, n_in, out_shape):
        return pl.pallas_call(
            kernel,
            out_shape=out_shape,
            grid_spec=pltpu.PrefetchScalarGridSpec(
                num_scalar_prefetch=1,
                grid=(1,),
                in_specs=[tile_spec(s) for s in strata] + in_vmem(n_in),
                out_specs=jax.tree.map(lambda _: pl.BlockSpec(memory_space=pltpu.VMEM), out_shape),
            ),
        )

    def padded(x):
        return jnp.pad(x, ((0, rows - x.shape[0]), (0, 0)))

    def pick(x, y):
        return jnp.where(core == 0, padded(x), padded(y))

    mine = pick(b, c)
    other = pick(c, b)
    before = pick(b + step_rate * vb, c + step_rate * vc)
    zshape = f32(kb, jb, rank)
    z = over_tiles(first_kernel, [0], 1, zshape)(order, tiles, a)
    for s in range(STRATA):
        b_now, c_now, send, keep = pl.pallas_call(
            functools.partial(gradient_kernel, mult_b=mult_b, mult_c=mult_c, parts=parts),
            out_shape=(f32(jb, rank), f32(kb, rank), f32(rows, rank), f32(rows, rank)),
            in_specs=[pl.BlockSpec(memory_space=pltpu.SMEM)] + in_vmem(5),
            out_specs=tuple(in_vmem(4)),
            scratch_shapes=[pltpu.VMEM((jb, rank), jnp.float32), pltpu.VMEM((kb, rank), jnp.float32)],
        )(core_arg, z, a, mine, other, before)
        summed = keep + swap(send)
        if s + 1 < STRATA:
            arrived = [onward(summed, turn) for turn in range(parts)]
            before = onward(mine, 0)
            a, va, z = over_tiles(
                functools.partial(window_kernel, scale=scale_a),
                [s, s + 1],
                4,
                (f32(ib, rank), f32(ib, rank), zshape),
            )(order, tiles, tiles, a, va, b_now, c_now)
            arrived, before, a, va, z = lax.optimization_barrier((arrived, before, a, va, z))
            mine = functools.reduce(jnp.add, arrived)
            other = swap(mine)
        else:
            arrived = [around(summed, turn) for turn in range(1, parts)]
            a = over_tiles(functools.partial(last_kernel, scale=scale_a), [s], 4, f32(ib, rank))(
                order, tiles, a, va, b_now, c_now
            )
            arrived, a = lax.optimization_barrier((arrived, a))
            mine = functools.reduce(jnp.add, arrived, summed)
            other = swap(mine)
    b_out = jnp.where(core == 0, mine[:jb], other[:jb])
    c_out = jnp.where(core == 0, other[:kb], mine[:kb])
    return a, b_out, c_out


def solution(mesh):
    return jax.shard_map(
        shards,
        mesh=mesh,
        in_specs=(
            P(None, None, BOTH, None),
            P(BOTH, None),
            P(BOTH, None),
            P("wide", None),
            P("wide", None),
            P(BOTH, None),
            P("wide", None),
            P("wide", None),
        ),
        out_specs=(P(BOTH, None), P("wide", None), P("wide", None)),
        check_vma=False,
    )
```

```python
import functools

import jax
import jax.numpy as jnp
from jax import lax
from jax.experimental import pallas as pl
from jax.experimental.pallas import tpu as pltpu
from jax.sharding import PartitionSpec as P


STRATA = 4
SECOND_STRIDE = 1
THIRD_STRIDE = 3
CORES = 2
STEP = 8

momentum = 0.9
step_rate = 20.0

BOTH = ("wide", "narrow")
GRANT = pltpu.CompilerParams(vmem_limit_bytes=20 << 20)
HBM = pl.BlockSpec(memory_space=pltpu.HBM)
VMEM = pl.BlockSpec(memory_space=pltpu.VMEM)
SMEM = pl.BlockSpec(memory_space=pltpu.SMEM)


def f32(*shape):
    return jax.ShapeDtypeStruct(shape, jnp.float32)


def in_hbm(x):
    return pltpu.with_memory_space_constraint(x, pltpu.HBM)


def halves(x):
    hi = x.astype(jnp.bfloat16)
    lo = (x - hi.astype(jnp.float32)).astype(jnp.bfloat16)
    return hi, lo


def dot(x, y, contract=((1,), (0,))):
    return lax.dot_general(x, y, (contract, ((), ())), preferred_element_type=jnp.float32)


def gram(x):
    hi, lo = halves(x)
    return dot(
        jnp.concatenate([hi, hi, lo], axis=0), jnp.concatenate([hi, lo, hi], axis=0), ((0,), (0,))
    )


def apply(x, g):
    xh, xl = halves(x)
    gh, gl = halves(g)
    return dot(xh, gh) + (dot(xh, gl) + dot(xl, gh))


def doubled(x):
    return jnp.concatenate([x, x], axis=1)


def split_rows(x):
    return jnp.concatenate(halves(x), axis=0)


def pair_weights(a):
    hi, lo = halves(a)
    zero = jnp.zeros_like(hi)
    left = jnp.concatenate([hi, zero, lo, zero], axis=0)
    right = jnp.concatenate([zero, hi, zero, lo], axis=0)
    return jnp.concatenate([left, right], axis=1)


def products(tile, at, weights):
    _, ib, jb = tile.shape
    rank = weights.shape[1] // 2
    turned = [tile[pl.ds(at + m, 2)].reshape(2 * ib, jb).T for m in range(0, STEP, 2)]
    z = dot(doubled(jnp.concatenate(turned, axis=0)), weights)
    return [z[m // 2 * jb : (m // 2 + 1) * jb, m % 2 * rank : (m % 2 + 1) * rank] for m in range(STEP)]


def slices_times_b(tile, at, stacked):
    _, ib, jb = tile.shape
    x = tile[pl.ds(at, STEP)].reshape(STEP * ib, jb)
    return dot(doubled(x), stacked).reshape(STEP, ib, stacked.shape[1])


def advance_a(tile, a, va, b, c, bc_gram, scale):
    kb, ib, _ = tile.shape
    stacked = split_rows(b[...])

    def body(n, acc):
        at = pl.multiple_of(n * STEP, STEP)
        y = slices_times_b(tile, at, stacked)
        cs = c[pl.ds(at, STEP), :]
        for m in range(STEP):
            acc = acc + y[m] * cs[m : m + 1]
        return acc

    seen = lax.fori_loop(0, kb // STEP, body, jnp.zeros((ib, a.shape[1]), jnp.float32), unroll=2)
    grad = apply(a[...], bc_gram[...]) - seen
    va_new = momentum * va[...] + grad * scale
    return a[...] - step_rate * va_new, va_new


def window_kernel(slot, tiles, old, a, va, b, c, bc_gram, new, a_out, va_out, ata, z, sem, *, scale, stratum):
    copy = pltpu.make_async_copy(tiles.at[slot[0, stratum]], new, sem)
    copy.start()
    a_new, va_new = advance_a(old, a, va, b, c, bc_gram, scale)
    a_out[...] = a_new
    va_out[...] = va_new
    ata[...] = gram(a_new)
    weights = pair_weights(a_new)
    copy.wait()

    def body(n, carry):
        at = pl.multiple_of(n * STEP, STEP)
        for m, zk in enumerate(products(new, at, weights)):
            z[at + m] = zk
        return carry

    lax.fori_loop(0, new.shape[0] // STEP, body, 0, unroll=2)


def last_kernel(old, a, va, b, c, bc_gram, a_out, *, scale):
    a_out[...] = advance_a(old, a, va, b, c, bc_gram, scale)[0]


def place(core, for_b, for_c, keep, send):
    half = for_b.shape[0] // CORES
    keep[half:] = for_c
    send[half:] = for_c

    @pl.when(core[0] == 0)
    def _():
        keep[:half] = for_b[:half]
        send[:half] = for_b[half:]

    @pl.when(core[0] != 0)
    def _():
        keep[:half] = for_b[half:]
        send[:half] = for_b[:half]


def first_kernel(
    core, slot, tiles, a_in, b_in, c_in, va_in, vb_in, vc_in, tile, a, b, c, va, bc_gram, keep, send,
    vb, vc, mb, mc, tile_sem, sem, *, mult_b, mult_c, chips,
):
    kb, _, jb = tile.shape
    rank = a.shape[1]
    chunks = tile_sem.shape[0]
    size = kb // chunks
    pairs = [(a_in, a), (b_in, b), (c_in, c), (va_in, va), (vb_in, vb), (vc_in, vc)]
    rest = [pltpu.make_async_copy(x, y, sem.at[n]) for n, (x, y) in enumerate(pairs)]
    for copy in rest:
        copy.start()
    source = tiles.at[slot[0, 0]]
    parts = [
        pltpu.make_async_copy(source.at[pl.ds(n * size, size)], tile.at[pl.ds(n * size, size)], tile_sem.at[n])
        for n in range(chunks)
    ]
    for copy in parts:
        copy.start()
    for copy in rest:
        copy.wait()
    a_gram = gram(a[...])
    drag = momentum * step_rate
    lead = jnp.where(core[0] == 0, 1.0 / chips, 0.0)
    b_gram, c_gram = gram(b[...]), gram(c[...])
    bc_gram[...] = b_gram * c_gram
    mb[...] = lead * (b[...] - drag * vb[...]) - mult_b * apply(b[...], a_gram * c_gram)
    base_c = (1.0 / chips - lead) * (c[...] - drag * vc[...]) - mult_c * apply(c[...], a_gram * b_gram)
    weights = pair_weights(a[...])

    def body(n, acc):
        at = pl.multiple_of(n * STEP, STEP)
        cs = c[pl.ds(at, STEP), :]
        rows = []
        for m, zk in enumerate(products(tile, at, weights)):
            acc = acc + zk * cs[m : m + 1]
            rows.append(jnp.sum(zk * b[...], axis=0, keepdims=True))
        mc[pl.ds(at, STEP), :] = jnp.concatenate(rows, axis=0)
        return acc

    acc = jnp.zeros((jb, rank), jnp.float32)
    for n, copy in enumerate(parts):
        copy.wait()
        acc = lax.fori_loop(n * size // STEP, (n + 1) * size // STEP, body, acc)
    place(core, mb[...] + mult_b * acc, base_c + mult_c * mc[...], keep, send)


def gradient_kernel(core, tile, z, a, ata, mine, other, b, c, now, bc_gram, keep, send, mb, mc, *, mult_b, mult_c):
    kb, jb, rank = z.shape
    half = jb // CORES
    first = core[0] == 0

    @pl.when(first)
    def _():
        b[:half] = mine[:half]
        b[half:] = other[:half]

    @pl.when(jnp.logical_not(first))
    def _():
        b[:half] = other[:half]
        b[half:] = mine[:half]

    c[...] = mine[half:] + other[half:]

    @pl.when(first)
    def _():
        now[...] = b[...]

    @pl.when(jnp.logical_not(first))
    def _():
        now[...] = jnp.zeros(now.shape, jnp.float32)
        now[:kb] = c[...]

    stacked = split_rows(b[...])
    a_rows = a[...]
    mb[...] = jnp.zeros((jb, rank), jnp.float32)

    def body(n, carry):
        at = pl.multiple_of(n * STEP, STEP)
        y = slices_times_b(tile, at, stacked)
        mc[pl.ds(at, STEP), :] = jnp.concatenate(
            [jnp.sum(y[m] * a_rows, axis=0, keepdims=True) for m in range(STEP)], axis=0
        )
        cs = c[pl.ds(at, STEP), :]
        for lo in range(0, jb, 32):
            rows = pl.ds(lo, 32)
            acc = mb[rows]
            for m in range(STEP):
                acc = acc + z[at + m, rows] * cs[m : m + 1]
            mb[rows] = acc
        return carry

    lax.fori_loop(0, kb // STEP, body, 0, unroll=2)
    b_rows, c_rows, a_gram = b[...], c[...], ata[...]
    b_gram, c_gram = gram(b_rows), gram(c_rows)
    bc_gram[...] = b_gram * c_gram
    for_b = mult_b * (mb[...] - apply(b_rows, a_gram * c_gram))
    for_c = mult_c * (mc[...] - apply(c_rows, a_gram * b_gram))
    place(core, for_b, for_c, keep, send)


def shards(tiles, slot, a, b, c, va, vb, vc):
    wide = lax.axis_size("wide")
    narrow = lax.axis_size("narrow")
    chips = narrow // CORES
    core = lax.axis_index("narrow") % CORES
    lead = core == 0
    ib, jb, kb = a.shape[0], b.shape[0], c.shape[0]
    rank = a.shape[1]
    half = jb // CORES
    scale_a = 1.0 / (jb * kb)
    mults = dict(
        mult_b=step_rate / (narrow * ib * kb), mult_c=step_rate / (narrow * ib * jb)
    )
    far = in_hbm(tiles)
    core_arg = core.astype(jnp.int32).reshape(1)

    def permute(x, where):
        route = []
        for w in range(wide):
            for n in range(narrow):
                to = where(n // CORES, n % CORES)
                if to is not None:
                    ahead, chip, unit = to
                    target = (w + ahead) % wide * narrow + chip % chips * CORES + unit % CORES
                    route.append((w * narrow + n, target))
        return lax.ppermute(x, BOTH, route)

    def swap(x):
        return permute(x, lambda y, u: (0, y, u + 1))

    turns = range(chips)
    thirds = [[t for t in turns if t % CORES == u] for u in range(CORES)]
    plan = [
        [("b", t) for t in turns] + [("c", t) for t in thirds[0]],
        [("c", t) for t in thirds[1]] + [("b", t) for t in turns],
    ]
    length = max(map(len, plan))
    plan = [p + [None] * (length - len(p)) for p in plan]

    def onward(total):
        part = {"b": total[:half], "c": total[half:]}
        ahead = {"b": SECOND_STRIDE, "c": THIRD_STRIDE}
        got = []
        for pair in zip(*plan, strict=True):
            kinds = [p and p[0] for p in pair]

            def where(y, u, pair=pair):
                return pair[u] and (ahead[pair[u][0]], y + pair[u][1], u)

            if kinds[0] == kinds[1] or None in kinds:
                message = part[kinds[0] or kinds[1]]
            else:
                message = jnp.where(lead, part[kinds[0]], part[kinds[1]])
            got.append(permute(message, where))
        return got

    def collect(got, kind):
        sums = []
        for u in range(CORES):
            terms = [x for x, pair in zip(got, zip(*plan)) if pair[u] and pair[u][0] == kind]
            sums.append(functools.reduce(jnp.add, terms) if terms else jnp.zeros_like(got[0]))
        return jnp.where(lead, sums[0], sums[1])

    def around(x):
        return [permute(x, lambda y, u, t=t: (0, y + t, u)) for t in range(1, chips)]

    def ordered(mine, other):
        return jnp.where(lead, jnp.concatenate([mine, other], axis=0), jnp.concatenate([other, mine], axis=0))

    tile_shape = jax.ShapeDtypeStruct((kb, ib, jb), tiles.dtype)
    block_a, block_b, block_c, share = f32(ib, rank), f32(jb, rank), f32(kb, rank), f32(half + kb, rank)

    grams = f32(rank, rank)

    def scratch(x):
        return pltpu.VMEM(x.shape, x.dtype)

    args = a, b, c, va, vb, vc
    tile, a, b, c, va, bc_gram, keep, send = pl.pallas_call(
        functools.partial(first_kernel, chips=chips, **mults),
        out_shape=(tile_shape, block_a, block_b, block_c, block_a, grams, share, share),
        in_specs=[SMEM, SMEM] + [HBM] * 7,
        out_specs=(VMEM,) * 8,
        scratch_shapes=[scratch(x) for x in (block_b, block_c, block_b, block_c)]
        + [pltpu.SemaphoreType.DMA((4,)), pltpu.SemaphoreType.DMA((6,))],
        compiler_params=GRANT,
    )(core_arg, slot, far, *map(in_hbm, args))
    now = jnp.where(lead, b, jnp.pad(c, ((0, jb - kb), (0, 0))))
    for s in range(STRATA):
        received = swap(send)
        total = keep + received
        total, now, tile, a, va, b, c, bc_gram = lax.optimization_barrier(
            (total, now, tile, a, va, b, c, bc_gram)
        )
        if s + 1 == STRATA:
            break
        got = onward(total)
        past = permute(now, lambda y, u: ((SECOND_STRIDE, THIRD_STRIDE)[u], y, u))
        tile, a, va, ata, z = pl.pallas_call(
            functools.partial(window_kernel, scale=scale_a, stratum=s + 1),
            out_shape=(tile_shape, block_a, block_a, grams, f32(kb, jb, rank)),
            in_specs=[SMEM, HBM] + [VMEM] * 6,
            out_specs=(VMEM,) * 5,
            scratch_shapes=[pltpu.SemaphoreType.DMA],
            compiler_params=GRANT,
        )(slot, far, tile, a, va, b, c, bc_gram)
        got, a, va, ata, z = lax.optimization_barrier((got, a, va, ata, z))
        mine = jnp.concatenate([collect(got, "b"), collect(got, "c")], axis=0)
        other = swap(mine)
        b, c, now, bc_gram, keep, send = pl.pallas_call(
            functools.partial(gradient_kernel, **mults),
            out_shape=(block_b, block_c, block_b, grams, share, share),
            in_specs=[SMEM] + [VMEM] * 6,
            out_specs=(VMEM,) * 6,
            scratch_shapes=[scratch(block_b), scratch(block_c)],
            compiler_params=GRANT,
        )(core_arg, tile, z, a, ata, mine, other)
        base = ((1.0 + momentum) * now - momentum * past) * (1.0 / chips)
        none = jnp.zeros((half, rank), jnp.float32)
        for_c = jnp.where(lead, 0.0, base[:kb])
        keep = keep + jnp.concatenate([jnp.where(lead, base[:half], none), for_c], axis=0)
        send = send + jnp.concatenate([jnp.where(lead, base[half:], none), for_c], axis=0)
    others = around(total)
    a = pl.pallas_call(
        functools.partial(last_kernel, scale=scale_a),
        out_shape=f32(ib, rank),
        in_specs=[VMEM] * 6,
        out_specs=VMEM,
        compiler_params=GRANT,
    )(tile, a, va, b, c, bc_gram)
    others, a = lax.optimization_barrier((others, a))
    total = functools.reduce(jnp.add, others, total)
    return a, ordered(total[:half], swap(total[:half])), total[half:]


def solution(mesh):
    return program(mesh)


def program(mesh):
    return jax.shard_map(
        shards,
        mesh=mesh,
        in_specs=(
            P(None, None, BOTH, None),
            P(BOTH, None),
            P(BOTH, None),
            P("wide", None),
            P("wide", None),
            P(BOTH, None),
            P("wide", None),
            P("wide", None),
        ),
        out_specs=(P(BOTH, None), P("wide", None), P("wide", None)),
        check_vma=False,
    )
```

```python
import functools

import jax
import jax.numpy as jnp
from jax import lax
from jax.experimental import pallas as pl
from jax.experimental.pallas import tpu as pltpu
from jax.sharding import PartitionSpec as P


STRATA = 4
SECOND_STRIDE = 1
THIRD_STRIDE = 3
CORES = 2
STEP = 8

momentum = 0.9
step_rate = 20.0

BOTH = ("wide", "narrow")
GRANT = pltpu.CompilerParams(vmem_limit_bytes=20 << 20)
HBM = pl.BlockSpec(memory_space=pltpu.HBM)
VMEM = pl.BlockSpec(memory_space=pltpu.VMEM)
SMEM = pl.BlockSpec(memory_space=pltpu.SMEM)


def f32(*shape):
    return jax.ShapeDtypeStruct(shape, jnp.float32)


def in_hbm(x):
    return pltpu.with_memory_space_constraint(x, pltpu.HBM)


def halves(x):
    hi = x.astype(jnp.bfloat16)
    lo = (x - hi.astype(jnp.float32)).astype(jnp.bfloat16)
    return hi, lo


def dot(x, y, contract=((1,), (0,))):
    return lax.dot_general(x, y, (contract, ((), ())), preferred_element_type=jnp.float32)


def gram(x):
    hi, lo = halves(x)
    return dot(
        jnp.concatenate([hi, hi, lo], axis=0), jnp.concatenate([hi, lo, hi], axis=0), ((0,), (0,))
    )


def apply(x, g):
    xh, xl = halves(x)
    gh, gl = halves(g)
    return dot(xh, gh) + (dot(xh, gl) + dot(xl, gh))


def doubled(x):
    return jnp.concatenate([x, x], axis=1)


def split_rows(x):
    return jnp.concatenate(halves(x), axis=0)


def pair_weights(a):
    hi, lo = halves(a)
    zero = jnp.zeros_like(hi)
    left = jnp.concatenate([hi, zero, lo, zero], axis=0)
    right = jnp.concatenate([zero, hi, zero, lo], axis=0)
    return jnp.concatenate([left, right], axis=1)


def products(tile, at, weights):
    _, ib, jb = tile.shape
    rank = weights.shape[1] // 2
    turned = [tile[pl.ds(at + m, 2)].reshape(2 * ib, jb).T for m in range(0, STEP, 2)]
    z = dot(doubled(jnp.concatenate(turned, axis=0)), weights)
    return [z[m // 2 * jb : (m // 2 + 1) * jb, m % 2 * rank : (m % 2 + 1) * rank] for m in range(STEP)]


def slices_times_b(tile, at, stacked):
    _, ib, jb = tile.shape
    x = tile[pl.ds(at, STEP)].reshape(STEP * ib, jb)
    return dot(doubled(x), stacked).reshape(STEP, ib, stacked.shape[1])


def advance_a(tile, a, va, b, c, bc_gram, scale):
    kb, ib, _ = tile.shape
    stacked = split_rows(b[...])

    def body(n, acc):
        at = pl.multiple_of(n * STEP, STEP)
        y = slices_times_b(tile, at, stacked)
        cs = c[pl.ds(at, STEP), :]
        for m in range(STEP):
            acc = acc + y[m] * cs[m : m + 1]
        return acc

    seen = lax.fori_loop(0, kb // STEP, body, jnp.zeros((ib, a.shape[1]), jnp.float32), unroll=2)
    grad = apply(a[...], bc_gram[...]) - seen
    va_new = momentum * va[...] + grad * scale
    return a[...] - step_rate * va_new, va_new


def window_kernel(
    slot_in, tiles, old, a, va, b, c, bc_gram, new, a_out, va_out, ata, z, slot, slot_sem, sem, *, scale, stratum
):
    order = pltpu.make_async_copy(slot_in, slot, slot_sem)
    order.start()
    order.wait()
    copy = pltpu.make_async_copy(tiles.at[slot[0, stratum]], new, sem)
    copy.start()
    a_new, va_new = advance_a(old, a, va, b, c, bc_gram, scale)
    a_out[...] = a_new
    va_out[...] = va_new
    ata[...] = gram(a_new)
    weights = pair_weights(a_new)
    copy.wait()

    def body(n, carry):
        at = pl.multiple_of(n * STEP, STEP)
        for m, zk in enumerate(products(new, at, weights)):
            z[at + m] = zk
        return carry

    lax.fori_loop(0, new.shape[0] // STEP, body, 0, unroll=2)


def last_kernel(old, a, va, b, c, bc_gram, a_out, *, scale):
    a_out[...] = advance_a(old, a, va, b, c, bc_gram, scale)[0]


def place(core, for_b, for_c, keep, send):
    half = for_b.shape[0] // CORES
    keep[half:] = for_c
    send[half:] = for_c

    @pl.when(core[0] == 0)
    def _():
        keep[:half] = for_b[:half]
        send[:half] = for_b[half:]

    @pl.when(core[0] != 0)
    def _():
        keep[:half] = for_b[half:]
        send[:half] = for_b[:half]


def first_kernel(
    core, chip, slot_in, tiles, a_in, b_in, c_in, va_in, vb_in, vc_in, tile, a, b, c, va, bc_gram, now, base, keep, send,
    vb, vc, mb, mc, acc, z, slot, tile_sem, sem, *, mult_b, mult_c,
):
    kb, _, jb = tile.shape
    rank = a.shape[1]
    chunks = tile_sem.shape[0]
    size = kb // chunks
    pairs = [(a_in, a), (b_in, b), (c_in, c), (va_in, va), (vb_in, vb), (vc_in, vc)]
    pairs = [(slot_in, slot)] + pairs
    rest = [pltpu.make_async_copy(x, y, sem.at[n]) for n, (x, y) in enumerate(pairs)]
    for copy in rest:
        copy.start()
    rest[0].wait()
    source = tiles.at[slot[0, 0]]
    parts = [
        pltpu.make_async_copy(source.at[pl.ds(n * size, size)], tile.at[pl.ds(n * size, size)], tile_sem.at[n])
        for n in range(chunks)
    ]
    for copy in parts:
        copy.start()
    for copy in rest[1:]:
        copy.wait()
    a_gram = gram(a[...])
    b_gram, c_gram = gram(b[...]), gram(c[...])
    bc_gram[...] = b_gram * c_gram
    mb[...] = mult_b * apply(b[...], a_gram * c_gram)
    less_c = mult_c * apply(c[...], a_gram * b_gram)
    half = jb // CORES
    drag = momentum * step_rate
    for u in range(CORES):

        @pl.when(jnp.logical_and(chip[0] == 0, core[0] == u))
        def _(own=slice(u * half, (u + 1) * half)):
            now[...] = b[own]
            base[...] = b[own] - drag * vb[own]

    @pl.when(chip[0] != 0)
    def _():
        now[...] = (1.0 / CORES) * c[...]
        base[...] = (1.0 / CORES) * (c[...] - drag * vc[...])

    weights = pair_weights(a[...])

    acc[...] = jnp.zeros((jb, rank), jnp.float32)

    def produce(n, slot_of):
        for m, zk in enumerate(products(tile, pl.multiple_of(n * STEP, STEP), weights)):
            z[slot_of, m] = zk

    def consume(n, slot_of):
        at = pl.multiple_of(n * STEP, STEP)
        cs = c[pl.ds(at, STEP), :]
        sums = [jnp.zeros((8, rank), jnp.float32)] * STEP
        for lo in range(0, jb, 32):
            rows = pl.ds(lo, 32)
            own, b_rows = acc[rows], b[rows]
            for m in range(STEP):
                zk = z[slot_of, m, rows]
                own = own + zk * cs[m : m + 1]
                sums[m] = sums[m] + jnp.sum((zk * b_rows).reshape(4, 8, rank), axis=0)
            acc[rows] = own
        mc[pl.ds(at, STEP), :] = jnp.concatenate([jnp.sum(x, axis=0, keepdims=True) for x in sums], axis=0)

    per = size // STEP
    parts[0].wait()
    produce(0, 0)
    for n in range(1, kb // STEP):
        if n % per == 0:
            parts[n // per].wait()
        produce(n, n % 2)
        consume(n - 1, (n - 1) % 2)
    consume(kb // STEP - 1, (kb // STEP - 1) % 2)
    place(core, mult_b * acc[...] - mb[...], mult_c * mc[...] - less_c, keep, send)


def gradient_kernel(core, tile, z, a, mine, other, b, c, keep, send, mb, mc, y_even, y_odd, *, mult_b, mult_c):
    kb, jb, rank = z.shape
    half = jb // CORES
    steps = kb // STEP
    first = core[0] == 0

    @pl.when(first)
    def _():
        b[:half] = mine[:half]
        b[half:] = other[:half]

    @pl.when(jnp.logical_not(first))
    def _():
        b[:half] = other[:half]
        b[half:] = mine[:half]

    c[...] = mine[half:] + other[half:]
    stacked = split_rows(b[...])
    a_rows = a[...]
    mb[...] = jnp.zeros((jb, rank), jnp.float32)

    def consume(n, y):
        at = pl.multiple_of(n * STEP, STEP)
        mc[pl.ds(at, STEP), :] = jnp.concatenate(
            [jnp.sum(y[m] * a_rows, axis=0, keepdims=True) for m in range(STEP)], axis=0
        )
        cs = c[pl.ds(at, STEP), :]
        for lo in range(0, jb, 32):
            rows = pl.ds(lo, 32)
            acc = mb[rows]
            for m in range(STEP):
                acc = acc + z[at + m, rows] * cs[m : m + 1]
            mb[rows] = acc

    def body(n, carry):
        y_odd[...] = slices_times_b(tile, pl.multiple_of((2 * n + 1) * STEP, STEP), stacked)
        consume(2 * n, y_even)
        after = jnp.minimum(2 * n + 2, steps - 1)
        y_even[...] = slices_times_b(tile, pl.multiple_of(after * STEP, STEP), stacked)
        consume(2 * n + 1, y_odd)
        return carry

    y_even[...] = slices_times_b(tile, 0, stacked)
    lax.fori_loop(0, steps // 2, body, 0)
    place(core, mult_b * mb[...], mult_c * mc[...], keep, send)


def terms_kernel(ata, ata_other, mine, b, c, bc_gram, terms, *, mult_b, mult_c):
    half = b.shape[0] // CORES
    c_rows = c[...]
    a_gram, b_gram, c_gram = ata[...] + ata_other[...], gram(b[...]), gram(c_rows)
    bc_gram[...] = b_gram * c_gram
    terms[:half] = mult_b * apply(mine[:half], a_gram * c_gram)
    terms[half:] = mult_c * apply(c_rows, a_gram * b_gram)


def final_kernel(core, total, beside, same, cross, b, c):
    half = beside.shape[0]
    whole, other = total[...], beside[...]
    for n in range(same.shape[0]):
        whole = whole + same[n]
        other = other + cross[n]
    c[...] = whole[half:]

    @pl.when(core[0] == 0)
    def _():
        b[:half] = whole[:half]
        b[half:] = other

    @pl.when(core[0] != 0)
    def _():
        b[:half] = other
        b[half:] = whole[:half]


def shards(tiles, slot, a, b, c, va, vb, vc):
    wide = lax.axis_size("wide")
    narrow = lax.axis_size("narrow")
    chips = narrow // CORES
    place_in = lax.axis_index("narrow").astype(jnp.int32)
    core, chip = place_in % CORES, place_in // CORES
    lead = core == 0
    ib, jb, kb = a.shape[0], b.shape[0], c.shape[0]
    rank = a.shape[1]
    half = jb // CORES
    scale_a = 1.0 / (jb * kb)
    mults = dict(
        mult_b=step_rate / (narrow * ib * kb), mult_c=step_rate / (narrow * ib * jb)
    )
    far, order = in_hbm(tiles), in_hbm(slot)
    pos = core.reshape(1), chip.reshape(1)
    assert chips > 1 and half == kb

    def permute(x, where):
        route = []
        for w in range(wide):
            for n in range(narrow):
                to = where(n // CORES, n % CORES)
                if to is not None:
                    ahead, chip, unit = to
                    target = (w + ahead) % wide * narrow + chip % chips * CORES + unit % CORES
                    route.append((w * narrow + n, target))
        return lax.ppermute(x, BOTH, route)

    def swap(x):
        return permute(x, lambda y, u: (0, y, u + 1))

    turns = range(chips)
    thirds = [[t for t in turns if t % CORES == u] for u in range(CORES)]
    plan = [
        [("b", t) for t in turns] + [("c", t) for t in thirds[0]],
        [("c", t) for t in thirds[1]] + [("b", t) for t in turns],
    ]
    length = max(map(len, plan))
    plan = [p + [None] * (length - len(p)) for p in plan]

    def onward(total):
        part = {"b": total[:half], "c": total[half:]}
        ahead = {"b": SECOND_STRIDE, "c": THIRD_STRIDE}
        got = []
        for pair in zip(*plan, strict=True):
            kinds = [p and p[0] for p in pair]

            def where(y, u, pair=pair):
                return pair[u] and (ahead[pair[u][0]], y + pair[u][1], u)

            if kinds[0] == kinds[1] or None in kinds:
                message = part[kinds[0] or kinds[1]]
            else:
                message = jnp.where(lead, part[kinds[0]], part[kinds[1]])
            got.append(permute(message, where))
        return got

    def collect(got, kind):
        sums = []
        for u in range(CORES):
            terms = [x for x, pair in zip(got, zip(*plan)) if pair[u] and pair[u][0] == kind]
            sums.append(functools.reduce(jnp.add, terms) if terms else jnp.zeros_like(got[0]))
        return jnp.where(lead, sums[0], sums[1])

    tile_shape = jax.ShapeDtypeStruct((kb, ib, jb), tiles.dtype)
    block_a, block_b, block_c, share = f32(ib, rank), f32(jb, rank), f32(kb, rank), f32(half + kb, rank)

    grams = f32(rank, rank)

    def scratch(x):
        return pltpu.VMEM(x.shape, x.dtype)

    slots = pltpu.SMEM(slot.shape, slot.dtype)
    args = a, b, c, va, vb, vc
    tile, a, b, c, va, bc_gram, now, base, keep, send = pl.pallas_call(
        functools.partial(first_kernel, **mults),
        out_shape=(tile_shape, block_a, block_b, block_c, block_a, grams, block_c, block_c, share, share),
        in_specs=[SMEM] * 2 + [HBM] * 8,
        out_specs=(VMEM,) * 10,
        scratch_shapes=[scratch(x) for x in (block_b, block_c, block_b, block_c, block_b, f32(2, STEP, jb, rank))]
        + [slots, pltpu.SemaphoreType.DMA((4,)), pltpu.SemaphoreType.DMA((7,))],
        compiler_params=GRANT,
    )(*pos, order, far, *map(in_hbm, args))
    none = jnp.zeros((half, rank), jnp.float32)

    def with_base(keep, send, base):
        for_b, for_c = jnp.where(chip == 0, base, none), jnp.where(chip == 1, base, none)
        return (
            keep + jnp.concatenate([for_b, for_c], axis=0),
            send + jnp.concatenate([none, for_c], axis=0),
        )

    def forward(x):
        return permute(x, lambda y, u: ((SECOND_STRIDE, THIRD_STRIDE)[y], y, u) if y < 2 else None)

    for s in range(STRATA):
        keep, send = with_base(keep, send, base)
        received = swap(send)
        if s == 0:
            past = forward(now)
        total = keep + received
        if s > 0:
            bc_gram, terms = pl.pallas_call(
                functools.partial(terms_kernel, **mults),
                out_shape=(grams, share),
                in_specs=[VMEM] * 5,
                out_specs=(VMEM,) * 2,
                compiler_params=GRANT,
            )(*ours, mine, b, c)
            total = total - terms
        total, tile, a, va, b, c, bc_gram = lax.optimization_barrier((total, tile, a, va, b, c, bc_gram))
        if s + 1 == STRATA:
            break
        got = onward(total)
        tile, a, va, ata, z = pl.pallas_call(
            functools.partial(window_kernel, scale=scale_a, stratum=s + 1),
            out_shape=(tile_shape, block_a, block_a, grams, f32(kb, jb, rank)),
            in_specs=[HBM] * 2 + [VMEM] * 6,
            out_specs=(VMEM,) * 5,
            scratch_shapes=[slots, pltpu.SemaphoreType.DMA, pltpu.SemaphoreType.DMA],
            compiler_params=GRANT,
        )(order, far, tile, a, va, b, c, bc_gram)
        ata_other = swap(ata)
        got, a, va, z = lax.optimization_barrier((got, a, va, z))
        ours = ata, ata_other
        mine = jnp.concatenate([collect(got, "b"), collect(got, "c")], axis=0)
        other = swap(mine)
        before = past
        if s + 2 < STRATA:
            past = forward(jnp.where(chip == 0, mine[:half], mine[half:]))
        b, c, keep, send = pl.pallas_call(
            functools.partial(gradient_kernel, **mults),
            out_shape=(block_b, block_c, share, share),
            in_specs=[SMEM] + [VMEM] * 5,
            out_specs=(VMEM,) * 4,
            scratch_shapes=[scratch(x) for x in (block_b, block_c) + (f32(STEP, ib, rank),) * 2],
            compiler_params=GRANT,
        )(pos[0], tile, z, a, mine, other)
        base = (1.0 + momentum) * jnp.where(chip == 0, mine[:half], (1.0 / CORES) * c) - momentum * before
    beside = swap(total[:half])
    same = [permute(total, lambda y, u, t=t: (0, y + t, u)) for t in range(1, chips)]
    cross = [permute(total[:half], lambda y, u, t=t: (0, y + t, u + 1)) for t in range(1, chips)]
    a = pl.pallas_call(
        functools.partial(last_kernel, scale=scale_a),
        out_shape=f32(ib, rank),
        in_specs=[VMEM] * 6,
        out_specs=VMEM,
        compiler_params=GRANT,
    )(tile, a, va, b, c, bc_gram)
    beside, same, cross, a = lax.optimization_barrier((beside, same, cross, a))
    b, c = pl.pallas_call(
        final_kernel,
        out_shape=(block_b, block_c),
        in_specs=[SMEM] + [VMEM] * 4,
        out_specs=(VMEM,) * 2,
        compiler_params=GRANT,
    )(pos[0], total, beside, jnp.stack(same), jnp.stack(cross))
    return a, b, c


def solution(mesh):
    return program(mesh)


def program(mesh):
    return jax.shard_map(
        shards,
        mesh=mesh,
        in_specs=(
            P(None, None, BOTH, None),
            P(BOTH, None),
            P(BOTH, None),
            P("wide", None),
            P("wide", None),
            P(BOTH, None),
            P("wide", None),
            P("wide", None),
        ),
        out_specs=(P(BOTH, None), P("wide", None), P("wide", None)),
        check_vma=False,
    )
```

```python
import functools

import jax
import jax.numpy as jnp
from jax import lax
from jax.experimental import pallas as pl
from jax.experimental.pallas import tpu as pltpu
from jax.sharding import PartitionSpec as P


STRATA = 4
SECOND_STRIDE = 1
THIRD_STRIDE = 3
CORES = 2
STEP = 8

momentum = 0.9
step_rate = 20.0

BOTH = ("wide", "narrow")
GRANT = pltpu.CompilerParams(vmem_limit_bytes=20 << 20)
HBM = pl.BlockSpec(memory_space=pltpu.HBM)
VMEM = pl.BlockSpec(memory_space=pltpu.VMEM)
SMEM = pl.BlockSpec(memory_space=pltpu.SMEM)


def f32(*shape):
    return jax.ShapeDtypeStruct(shape, jnp.float32)


def in_hbm(x):
    return pltpu.with_memory_space_constraint(x, pltpu.HBM)


def halves(x):
    hi = x.astype(jnp.bfloat16)
    lo = (x - hi.astype(jnp.float32)).astype(jnp.bfloat16)
    return hi, lo


def dot(x, y, contract=((1,), (0,))):
    return lax.dot_general(x, y, (contract, ((), ())), preferred_element_type=jnp.float32)


def gram(x):
    hi, lo = halves(x)
    return dot(
        jnp.concatenate([hi, hi, lo], axis=0), jnp.concatenate([hi, lo, hi], axis=0), ((0,), (0,))
    )


def apply(x, g):
    xh, xl = halves(x)
    gh, gl = halves(g)
    return dot(xh, gh) + (dot(xh, gl) + dot(xl, gh))


def doubled(x):
    return jnp.concatenate([x, x], axis=1)


def split_rows(x):
    return jnp.concatenate(halves(x), axis=0)


def pair_weights(a):
    hi, lo = halves(a)
    zero = jnp.zeros_like(hi)
    left = jnp.concatenate([hi, zero, lo, zero], axis=0)
    right = jnp.concatenate([zero, hi, zero, lo], axis=0)
    return jnp.concatenate([left, right], axis=1)


def products(tile, at, weights):
    _, ib, jb = tile.shape
    rank = weights.shape[1] // 2
    turned = [tile[pl.ds(at + m, 2)].reshape(2 * ib, jb).T for m in range(0, STEP, 2)]
    z = dot(doubled(jnp.concatenate(turned, axis=0)), weights)
    return [z[m // 2 * jb : (m // 2 + 1) * jb, m % 2 * rank : (m % 2 + 1) * rank] for m in range(STEP)]


def slices_times_b(tile, at, stacked):
    _, ib, jb = tile.shape
    x = tile[pl.ds(at, STEP)].reshape(STEP * ib, jb)
    return dot(doubled(x), stacked).reshape(STEP, ib, stacked.shape[1])


def advance_a(tile, a, va, b, c, bc_gram, scale, midway=None):
    kb, ib, _ = tile.shape
    stacked = split_rows(b[...])

    def body(n, acc):
        at = pl.multiple_of(n * STEP, STEP)
        y = slices_times_b(tile, at, stacked)
        cs = c[pl.ds(at, STEP), :]
        for m in range(STEP):
            acc = acc + y[m] * cs[m : m + 1]
        return acc

    early = 2
    seen = lax.fori_loop(0, early, body, jnp.zeros((ib, a.shape[1]), jnp.float32), unroll=2)
    if midway is not None:
        midway()
    seen = lax.fori_loop(early, kb // STEP, body, seen, unroll=2)
    grad = apply(a[...], bc_gram[...]) - seen
    va_new = momentum * va[...] + grad * scale
    return a[...] - step_rate * va_new, va_new


def window_kernel(
    slot_in, tiles, old, a, va, b, c, bc_gram, new, a_out, va_out, ata, z, slot, slot_sem, sem, *, scale, stratum
):
    order = pltpu.make_async_copy(slot_in, slot, slot_sem)
    order.start()

    def fetch():
        order.wait()
        pltpu.make_async_copy(tiles.at[slot[0, stratum]], new, sem).start()

    a_new, va_new = advance_a(old, a, va, b, c, bc_gram, scale, fetch)
    a_out[...] = a_new
    va_out[...] = va_new
    ata[...] = gram(a_new)
    weights = pair_weights(a_new)
    pltpu.make_async_copy(tiles.at[slot[0, stratum]], new, sem).wait()

    def body(n, carry):
        at = pl.multiple_of(n * STEP, STEP)
        for m, zk in enumerate(products(new, at, weights)):
            z[at + m] = zk
        return carry

    lax.fori_loop(0, new.shape[0] // STEP, body, 0, unroll=4)


def last_kernel(old, a, va, b, c, bc_gram, a_out, *, scale):
    a_out[...] = advance_a(old, a, va, b, c, bc_gram, scale)[0]


def place(core, for_b, for_c, keep, send):
    half = for_b.shape[0] // CORES
    keep[half:] = for_c
    send[half:] = for_c

    @pl.when(core[0] == 0)
    def _():
        keep[:half] = for_b[:half]
        send[:half] = for_b[half:]

    @pl.when(core[0] != 0)
    def _():
        keep[:half] = for_b[half:]
        send[:half] = for_b[:half]


def first_kernel(
    core, chip, slot_in, tiles, a_in, b_in, c_in, va_in, vb_in, vc_in, tile, a, b, c, va, bc_gram, now, base, keep, send,
    vb, vc, mb, mc, acc, z, slot, tile_sem, sem, *, mult_b, mult_c,
):
    kb, _, jb = tile.shape
    rank = a.shape[1]
    chunks = tile_sem.shape[0]
    size = kb // chunks
    pairs = [(a_in, a), (b_in, b), (c_in, c), (va_in, va), (vb_in, vb), (vc_in, vc)]
    pairs = [(slot_in, slot)] + pairs
    rest = [pltpu.make_async_copy(x, y, sem.at[n]) for n, (x, y) in enumerate(pairs)]
    for copy in rest:
        copy.start()
    rest[0].wait()
    source = tiles.at[slot[0, 0]]
    parts = [
        pltpu.make_async_copy(source.at[pl.ds(n * size, size)], tile.at[pl.ds(n * size, size)], tile_sem.at[n])
        for n in range(chunks)
    ]
    for copy in parts:
        copy.start()
    for copy in rest[1:]:
        copy.wait()
    a_gram = gram(a[...])
    b_gram, c_gram = gram(b[...]), gram(c[...])
    bc_gram[...] = b_gram * c_gram
    mb[...] = mult_b * apply(b[...], a_gram * c_gram)
    less_c = mult_c * apply(c[...], a_gram * b_gram)
    half = jb // CORES
    drag = momentum * step_rate
    for u in range(CORES):

        @pl.when(jnp.logical_and(chip[0] == 0, core[0] == u))
        def _(own=slice(u * half, (u + 1) * half)):
            now[...] = b[own]
            base[...] = b[own] - drag * vb[own]

    @pl.when(chip[0] != 0)
    def _():
        now[...] = (1.0 / CORES) * c[...]
        base[...] = (1.0 / CORES) * (c[...] - drag * vc[...])

    weights = pair_weights(a[...])

    acc[...] = jnp.zeros((jb, rank), jnp.float32)

    def produce(n, slot_of):
        for m, zk in enumerate(products(tile, pl.multiple_of(n * STEP, STEP), weights)):
            z[slot_of, m] = zk

    def consume(n, slot_of):
        at = pl.multiple_of(n * STEP, STEP)
        cs = c[pl.ds(at, STEP), :]
        sums = [jnp.zeros((8, rank), jnp.float32)] * STEP
        for lo in range(0, jb, 32):
            rows = pl.ds(lo, 32)
            own, b_rows = acc[rows], b[rows]
            for m in range(STEP):
                zk = z[slot_of, m, rows]
                own = own + zk * cs[m : m + 1]
                sums[m] = sums[m] + jnp.sum((zk * b_rows).reshape(4, 8, rank), axis=0)
            acc[rows] = own
        mc[pl.ds(at, STEP), :] = jnp.concatenate([jnp.sum(x, axis=0, keepdims=True) for x in sums], axis=0)

    per = size // STEP
    parts[0].wait()
    produce(0, 0)
    for n in range(1, kb // STEP):
        if n % per == 0:
            parts[n // per].wait()
        produce(n, n % 2)
        consume(n - 1, (n - 1) % 2)
    consume(kb // STEP - 1, (kb // STEP - 1) % 2)
    place(core, mult_b * acc[...] - mb[...], mult_c * mc[...] - less_c, keep, send)


def gradient_kernel(core, tile, z, a, mine, other, b, c, keep, send, mb, mc, y_even, y_odd, *, mult_b, mult_c):
    kb, jb, rank = z.shape
    half = jb // CORES
    steps = kb // STEP
    first = core[0] == 0

    @pl.when(first)
    def _():
        b[:half] = mine[:half]
        b[half:] = other[:half]

    @pl.when(jnp.logical_not(first))
    def _():
        b[:half] = other[:half]
        b[half:] = mine[:half]

    c[...] = mine[half:] + other[half:]
    stacked = split_rows(b[...])
    a_rows = a[...]
    mb[...] = jnp.zeros((jb, rank), jnp.float32)

    def consume(n, y):
        at = pl.multiple_of(n * STEP, STEP)
        mc[pl.ds(at, STEP), :] = jnp.concatenate(
            [jnp.sum(y[m] * a_rows, axis=0, keepdims=True) for m in range(STEP)], axis=0
        )
        cs = c[pl.ds(at, STEP), :]
        for lo in range(0, jb, 32):
            rows = pl.ds(lo, 32)
            acc = mb[rows]
            for m in range(STEP):
                acc = acc + z[at + m, rows] * cs[m : m + 1]
            mb[rows] = acc

    def body(n, carry):
        y_odd[...] = slices_times_b(tile, pl.multiple_of((2 * n + 1) * STEP, STEP), stacked)
        consume(2 * n, y_even)
        after = jnp.minimum(2 * n + 2, steps - 1)
        y_even[...] = slices_times_b(tile, pl.multiple_of(after * STEP, STEP), stacked)
        consume(2 * n + 1, y_odd)
        return carry

    y_even[...] = slices_times_b(tile, 0, stacked)
    lax.fori_loop(0, steps // 2, body, 0, unroll=2)
    place(core, mult_b * mb[...], mult_c * mc[...], keep, send)


def terms_kernel(ata, ata_other, mine, b, c, bc_gram, terms, *, mult_b, mult_c):
    half = b.shape[0] // CORES
    c_rows = c[...]
    a_gram, b_gram, c_gram = ata[...] + ata_other[...], gram(b[...]), gram(c_rows)
    bc_gram[...] = b_gram * c_gram
    terms[:half] = mult_b * apply(mine[:half], a_gram * c_gram)
    terms[half:] = mult_c * apply(c_rows, a_gram * b_gram)


def final_kernel(core, total, beside, same, cross, b, c):
    half = beside.shape[0]
    whole, other = total[...], beside[...]
    for n in range(same.shape[0]):
        whole = whole + same[n]
        other = other + cross[n]
    c[...] = whole[half:]

    @pl.when(core[0] == 0)
    def _():
        b[:half] = whole[:half]
        b[half:] = other

    @pl.when(core[0] != 0)
    def _():
        b[:half] = other
        b[half:] = whole[:half]


def shards(tiles, slot, a, b, c, va, vb, vc):
    wide = lax.axis_size("wide")
    narrow = lax.axis_size("narrow")
    chips = narrow // CORES
    place_in = lax.axis_index("narrow").astype(jnp.int32)
    core, chip = place_in % CORES, place_in // CORES
    lead = core == 0
    ib, jb, kb = a.shape[0], b.shape[0], c.shape[0]
    rank = a.shape[1]
    half = jb // CORES
    scale_a = 1.0 / (jb * kb)
    mults = dict(
        mult_b=step_rate / (narrow * ib * kb), mult_c=step_rate / (narrow * ib * jb)
    )
    far, order = in_hbm(tiles), in_hbm(slot)
    pos = core.reshape(1), chip.reshape(1)
    assert chips > 1 and half == kb

    def permute(x, where):
        route = []
        for w in range(wide):
            for n in range(narrow):
                to = where(n // CORES, n % CORES)
                if to is not None:
                    ahead, chip, unit = to
                    target = (w + ahead) % wide * narrow + chip % chips * CORES + unit % CORES
                    route.append((w * narrow + n, target))
        return lax.ppermute(x, BOTH, route)

    def swap(x):
        return permute(x, lambda y, u: (0, y, u + 1))

    turns = range(chips)
    thirds = [[t for t in turns if t % CORES == u] for u in range(CORES)]
    plan = [
        [("b", t) for t in turns] + [("c", t) for t in thirds[0]],
        [("c", t) for t in thirds[1]] + [("b", t) for t in turns],
    ]
    length = max(map(len, plan))
    plan = [p + [None] * (length - len(p)) for p in plan]

    def onward(total):
        part = {"b": total[:half], "c": total[half:]}
        ahead = {"b": SECOND_STRIDE, "c": THIRD_STRIDE}
        got = []
        for pair in zip(*plan, strict=True):
            kinds = [p and p[0] for p in pair]

            def where(y, u, pair=pair):
                return pair[u] and (ahead[pair[u][0]], y + pair[u][1], u)

            if kinds[0] == kinds[1] or None in kinds:
                message = part[kinds[0] or kinds[1]]
            else:
                message = jnp.where(lead, part[kinds[0]], part[kinds[1]])
            got.append(permute(message, where))
        return got

    def collect(got, kind):
        sums = []
        for u in range(CORES):
            terms = [x for x, pair in zip(got, zip(*plan)) if pair[u] and pair[u][0] == kind]
            sums.append(functools.reduce(jnp.add, terms) if terms else jnp.zeros_like(got[0]))
        return jnp.where(lead, sums[0], sums[1])

    tile_shape = jax.ShapeDtypeStruct((kb, ib, jb), tiles.dtype)
    block_a, block_b, block_c, share = f32(ib, rank), f32(jb, rank), f32(kb, rank), f32(half + kb, rank)

    grams = f32(rank, rank)

    def scratch(x):
        return pltpu.VMEM(x.shape, x.dtype)

    slots = pltpu.SMEM(slot.shape, slot.dtype)
    args = a, b, c, va, vb, vc
    tile, a, b, c, va, bc_gram, now, base, keep, send = pl.pallas_call(
        functools.partial(first_kernel, **mults),
        out_shape=(tile_shape, block_a, block_b, block_c, block_a, grams, block_c, block_c, share, share),
        in_specs=[SMEM] * 2 + [HBM] * 8,
        out_specs=(VMEM,) * 10,
        scratch_shapes=[scratch(x) for x in (block_b, block_c, block_b, block_c, block_b, f32(2, STEP, jb, rank))]
        + [slots, pltpu.SemaphoreType.DMA((4,)), pltpu.SemaphoreType.DMA((7,))],
        compiler_params=GRANT,
    )(*pos, order, far, *map(in_hbm, args))
    none = jnp.zeros((half, rank), jnp.float32)

    def with_base(keep, send, base):
        for_b, for_c = jnp.where(chip == 0, base, none), jnp.where(chip == 1, base, none)
        return (
            keep + jnp.concatenate([for_b, for_c], axis=0),
            send + jnp.concatenate([none, for_c], axis=0),
        )

    def forward(x):
        return permute(x, lambda y, u: ((SECOND_STRIDE, THIRD_STRIDE)[y], y, u) if y < 2 else None)

    for s in range(STRATA):
        keep, send = with_base(keep, send, base)
        received = swap(send)
        if s == 0:
            past = forward(now)
        total = keep + received
        if s > 0:
            bc_gram, terms = pl.pallas_call(
                functools.partial(terms_kernel, **mults),
                out_shape=(grams, share),
                in_specs=[VMEM] * 5,
                out_specs=(VMEM,) * 2,
                compiler_params=GRANT,
            )(*ours, mine, b, c)
            total = total - terms
        total, tile, a, va, b, c, bc_gram = lax.optimization_barrier((total, tile, a, va, b, c, bc_gram))
        if s + 1 == STRATA:
            break
        got = onward(total)
        tile, a, va, ata, z = pl.pallas_call(
            functools.partial(window_kernel, scale=scale_a, stratum=s + 1),
            out_shape=(tile_shape, block_a, block_a, grams, f32(kb, jb, rank)),
            in_specs=[HBM] * 2 + [VMEM] * 6,
            out_specs=(VMEM,) * 5,
            scratch_shapes=[slots, pltpu.SemaphoreType.DMA, pltpu.SemaphoreType.DMA],
            compiler_params=GRANT,
        )(order, far, tile, a, va, b, c, bc_gram)
        ata_other = swap(ata)
        got, a, va, z = lax.optimization_barrier((got, a, va, z))
        ours = ata, ata_other
        mine = jnp.concatenate([collect(got, "b"), collect(got, "c")], axis=0)
        other = swap(mine)
        before = past
        if s + 2 < STRATA:
            past = forward(jnp.where(chip == 0, mine[:half], mine[half:]))
        b, c, keep, send = pl.pallas_call(
            functools.partial(gradient_kernel, **mults),
            out_shape=(block_b, block_c, share, share),
            in_specs=[SMEM] + [VMEM] * 5,
            out_specs=(VMEM,) * 4,
            scratch_shapes=[scratch(x) for x in (block_b, block_c) + (f32(STEP, ib, rank),) * 2],
            compiler_params=GRANT,
        )(pos[0], tile, z, a, mine, other)
        base = (1.0 + momentum) * jnp.where(chip == 0, mine[:half], (1.0 / CORES) * c) - momentum * before
    beside = swap(total[:half])
    same = [permute(total, lambda y, u, t=t: (0, y + t, u)) for t in range(1, chips)]
    cross = [permute(total[:half], lambda y, u, t=t: (0, y + t, u + 1)) for t in range(1, chips)]
    a = pl.pallas_call(
        functools.partial(last_kernel, scale=scale_a),
        out_shape=f32(ib, rank),
        in_specs=[VMEM] * 6,
        out_specs=VMEM,
        compiler_params=GRANT,
    )(tile, a, va, b, c, bc_gram)
    beside, same, cross, a = lax.optimization_barrier((beside, same, cross, a))
    b, c = pl.pallas_call(
        final_kernel,
        out_shape=(block_b, block_c),
        in_specs=[SMEM] + [VMEM] * 4,
        out_specs=(VMEM,) * 2,
        compiler_params=GRANT,
    )(pos[0], total, beside, jnp.stack(same), jnp.stack(cross))
    return a, b, c


def solution(mesh):
    return program(mesh)


def program(mesh):
    return jax.shard_map(
        shards,
        mesh=mesh,
        in_specs=(
            P(None, None, BOTH, None),
            P(BOTH, None),
            P(BOTH, None),
            P("wide", None),
            P("wide", None),
            P(BOTH, None),
            P("wide", None),
            P("wide", None),
        ),
        out_specs=(P(BOTH, None), P("wide", None), P("wide", None)),
        check_vma=False,
    )
```

```python
import functools

import jax
import jax.numpy as jnp
from jax import lax
from jax.experimental import pallas as pl
from jax.experimental.pallas import tpu as pltpu
from jax.sharding import PartitionSpec as P


STRATA = 4
SECOND_STRIDE = 1
THIRD_STRIDE = 3
CORES = 2
STEP = 8

momentum = 0.9
step_rate = 20.0

BOTH = ("wide", "narrow")
GRANT = pltpu.CompilerParams(vmem_limit_bytes=20 << 20)
HBM = pl.BlockSpec(memory_space=pltpu.HBM)
VMEM = pl.BlockSpec(memory_space=pltpu.VMEM)
SMEM = pl.BlockSpec(memory_space=pltpu.SMEM)


def f32(*shape):
    return jax.ShapeDtypeStruct(shape, jnp.float32)


def in_hbm(x):
    return pltpu.with_memory_space_constraint(x, pltpu.HBM)


def halves(x):
    hi = x.astype(jnp.bfloat16)
    lo = (x - hi.astype(jnp.float32)).astype(jnp.bfloat16)
    return hi, lo


def dot(x, y, contract=((1,), (0,))):
    return lax.dot_general(x, y, (contract, ((), ())), preferred_element_type=jnp.float32)


def gram(x):
    hi, lo = halves(x)
    return dot(
        jnp.concatenate([hi, hi, lo], axis=0), jnp.concatenate([hi, lo, hi], axis=0), ((0,), (0,))
    )


def apply(x, g):
    xh, xl = halves(x)
    gh, gl = halves(g)
    return dot(xh, gh) + (dot(xh, gl) + dot(xl, gh))


def doubled(x):
    return jnp.concatenate([x, x], axis=1)


def split_rows(x):
    return jnp.concatenate(halves(x), axis=0)


def pair_weights(a):
    hi, lo = halves(a)
    zero = jnp.zeros_like(hi)
    left = jnp.concatenate([hi, zero, lo, zero], axis=0)
    right = jnp.concatenate([zero, hi, zero, lo], axis=0)
    return jnp.concatenate([left, right], axis=1)


def products(tile, at, weights):
    _, ib, jb = tile.shape
    rank = weights.shape[1] // 2
    turned = [tile[pl.ds(at + m, 2)].reshape(2 * ib, jb).T for m in range(0, STEP, 2)]
    z = dot(doubled(jnp.concatenate(turned, axis=0)), weights)
    return [z[m // 2 * jb : (m // 2 + 1) * jb, m % 2 * rank : (m % 2 + 1) * rank] for m in range(STEP)]


def slices_times_b(tile, at, stacked):
    _, ib, jb = tile.shape
    x = tile[pl.ds(at, STEP)].reshape(STEP * ib, jb)
    return dot(doubled(x), stacked).reshape(STEP, ib, stacked.shape[1])


def advance_a(tile, a, va, b, c, bc_gram, scale, midway=None):
    kb, ib, _ = tile.shape
    stacked = split_rows(b[...])

    def body(n, acc):
        at = pl.multiple_of(n * STEP, STEP)
        y = slices_times_b(tile, at, stacked)
        cs = c[pl.ds(at, STEP), :]
        for m in range(STEP):
            acc = acc + y[m] * cs[m : m + 1]
        return acc

    early = 2
    seen = lax.fori_loop(0, early, body, jnp.zeros((ib, a.shape[1]), jnp.float32), unroll=2)
    if midway is not None:
        midway()
    seen = lax.fori_loop(early, kb // STEP, body, seen, unroll=kb // STEP - early)
    grad = apply(a[...], bc_gram[...]) - seen
    va_new = momentum * va[...] + grad * scale
    return a[...] - step_rate * va_new, va_new


def window_kernel(
    slot_in, tiles, old, a, va, b, c, bc_gram, new, a_out, va_out, ata, z, slot, slot_sem, sem, *, scale, stratum
):
    order = pltpu.make_async_copy(slot_in, slot, slot_sem)
    order.start()

    def fetch():
        order.wait()
        pltpu.make_async_copy(tiles.at[slot[0, stratum]], new, sem).start()

    a_new, va_new = advance_a(old, a, va, b, c, bc_gram, scale, fetch)
    a_out[...] = a_new
    va_out[...] = va_new
    ata[...] = gram(a_new)
    weights = pair_weights(a_new)
    pltpu.make_async_copy(tiles.at[slot[0, stratum]], new, sem).wait()

    def body(n, carry):
        at = pl.multiple_of(n * STEP, STEP)
        for m, zk in enumerate(products(new, at, weights)):
            z[at + m] = zk
        return carry

    lax.fori_loop(0, new.shape[0] // STEP, body, 0, unroll=new.shape[0] // STEP)


def last_kernel(old, a, va, b, c, bc_gram, a_out, *, scale):
    a_out[...] = advance_a(old, a, va, b, c, bc_gram, scale)[0]


def place(core, for_b, for_c, keep, send):
    half = for_b.shape[0] // CORES
    keep[half:] = for_c
    send[half:] = for_c

    @pl.when(core[0] == 0)
    def _():
        keep[:half] = for_b[:half]
        send[:half] = for_b[half:]

    @pl.when(core[0] != 0)
    def _():
        keep[:half] = for_b[half:]
        send[:half] = for_b[:half]


def first_kernel(
    core, chip, slot_in, tiles, a_in, b_in, c_in, va_in, vb_in, vc_in, tile, a, b, c, va, bc_gram, now, base, keep, send,
    vb, vc, mb, mc, acc, z, slot, tile_sem, sem, *, mult_b, mult_c,
):
    kb, _, jb = tile.shape
    rank = a.shape[1]
    chunks = tile_sem.shape[0]
    size = kb // chunks
    pairs = [(a_in, a), (b_in, b), (c_in, c), (va_in, va), (vb_in, vb), (vc_in, vc)]
    pairs = [(slot_in, slot)] + pairs
    rest = [pltpu.make_async_copy(x, y, sem.at[n]) for n, (x, y) in enumerate(pairs)]
    for copy in rest:
        copy.start()
    rest[0].wait()
    source = tiles.at[slot[0, 0]]
    parts = [
        pltpu.make_async_copy(source.at[pl.ds(n * size, size)], tile.at[pl.ds(n * size, size)], tile_sem.at[n])
        for n in range(chunks)
    ]
    for copy in parts:
        copy.start()
    for copy in rest[1:]:
        copy.wait()
    a_gram = gram(a[...])
    b_gram, c_gram = gram(b[...]), gram(c[...])
    bc_gram[...] = b_gram * c_gram
    mb[...] = mult_b * apply(b[...], a_gram * c_gram)
    less_c = mult_c * apply(c[...], a_gram * b_gram)
    half = jb // CORES
    drag = momentum * step_rate
    for u in range(CORES):

        @pl.when(jnp.logical_and(chip[0] == 0, core[0] == u))
        def _(own=slice(u * half, (u + 1) * half)):
            now[...] = b[own]
            base[...] = b[own] - drag * vb[own]

    @pl.when(chip[0] != 0)
    def _():
        now[...] = (1.0 / CORES) * c[...]
        base[...] = (1.0 / CORES) * (c[...] - drag * vc[...])

    weights = pair_weights(a[...])

    acc[...] = jnp.zeros((jb, rank), jnp.float32)

    def produce(n, slot_of):
        for m, zk in enumerate(products(tile, pl.multiple_of(n * STEP, STEP), weights)):
            z[slot_of, m] = zk

    def consume(n, slot_of):
        at = pl.multiple_of(n * STEP, STEP)
        cs = c[pl.ds(at, STEP), :]
        sums = [jnp.zeros((8, rank), jnp.float32)] * STEP
        for lo in range(0, jb, 32):
            rows = pl.ds(lo, 32)
            own, b_rows = acc[rows], b[rows]
            for m in range(STEP):
                zk = z[slot_of, m, rows]
                own = own + zk * cs[m : m + 1]
                sums[m] = sums[m] + jnp.sum((zk * b_rows).reshape(4, 8, rank), axis=0)
            acc[rows] = own
        mc[pl.ds(at, STEP), :] = jnp.concatenate([jnp.sum(x, axis=0, keepdims=True) for x in sums], axis=0)

    per = size // STEP
    parts[0].wait()
    produce(0, 0)
    for n in range(1, kb // STEP):
        if n % per == 0:
            parts[n // per].wait()
        produce(n, n % 2)
        consume(n - 1, (n - 1) % 2)
    consume(kb // STEP - 1, (kb // STEP - 1) % 2)
    place(core, mult_b * acc[...] - mb[...], mult_c * mc[...] - less_c, keep, send)


def gradient_kernel(core, tile, z, a, mine, other, b, c, keep, send, mb, mc, y_even, y_odd, *, mult_b, mult_c):
    kb, jb, rank = z.shape
    half = jb // CORES
    steps = kb // STEP
    first = core[0] == 0

    @pl.when(first)
    def _():
        b[:half] = mine[:half]
        b[half:] = other[:half]

    @pl.when(jnp.logical_not(first))
    def _():
        b[:half] = other[:half]
        b[half:] = mine[:half]

    c[...] = mine[half:] + other[half:]
    stacked = split_rows(b[...])
    a_rows = a[...]
    mb[...] = jnp.zeros((jb, rank), jnp.float32)

    def consume(n, y):
        at = pl.multiple_of(n * STEP, STEP)
        mc[pl.ds(at, STEP), :] = jnp.concatenate(
            [jnp.sum(y[m] * a_rows, axis=0, keepdims=True) for m in range(STEP)], axis=0
        )
        cs = c[pl.ds(at, STEP), :]
        for lo in range(0, jb, 32):
            rows = pl.ds(lo, 32)
            acc = mb[rows]
            for m in range(STEP):
                acc = acc + z[at + m, rows] * cs[m : m + 1]
            mb[rows] = acc

    def body(n, carry):
        y_odd[...] = slices_times_b(tile, pl.multiple_of((2 * n + 1) * STEP, STEP), stacked)
        consume(2 * n, y_even)
        after = jnp.minimum(2 * n + 2, steps - 1)
        y_even[...] = slices_times_b(tile, pl.multiple_of(after * STEP, STEP), stacked)
        consume(2 * n + 1, y_odd)
        return carry

    y_even[...] = slices_times_b(tile, 0, stacked)
    lax.fori_loop(0, steps // 2, body, 0, unroll=steps // 2)
    place(core, mult_b * mb[...], mult_c * mc[...], keep, send)


def terms_kernel(ata, ata_other, mine, b, c, bc_gram, terms, *, mult_b, mult_c):
    half = b.shape[0] // CORES
    c_rows = c[...]
    a_gram, b_gram, c_gram = ata[...] + ata_other[...], gram(b[...]), gram(c_rows)
    bc_gram[...] = b_gram * c_gram
    terms[:half] = mult_b * apply(mine[:half], a_gram * c_gram)
    terms[half:] = mult_c * apply(c_rows, a_gram * b_gram)


def final_kernel(core, total, beside, same, cross, b, c):
    half = beside.shape[0]
    whole, other = total[...], beside[...]
    for n in range(same.shape[0]):
        whole = whole + same[n]
        other = other + cross[n]
    c[...] = whole[half:]

    @pl.when(core[0] == 0)
    def _():
        b[:half] = whole[:half]
        b[half:] = other

    @pl.when(core[0] != 0)
    def _():
        b[:half] = other
        b[half:] = whole[:half]


def shards(tiles, slot, a, b, c, va, vb, vc):
    wide = lax.axis_size("wide")
    narrow = lax.axis_size("narrow")
    chips = narrow // CORES
    place_in = lax.axis_index("narrow").astype(jnp.int32)
    core, chip = place_in % CORES, place_in // CORES
    lead = core == 0
    ib, jb, kb = a.shape[0], b.shape[0], c.shape[0]
    rank = a.shape[1]
    half = jb // CORES
    scale_a = 1.0 / (jb * kb)
    mults = dict(
        mult_b=step_rate / (narrow * ib * kb), mult_c=step_rate / (narrow * ib * jb)
    )
    far, order = in_hbm(tiles), in_hbm(slot)
    pos = core.reshape(1), chip.reshape(1)
    assert chips > 1 and half == kb

    def permute(x, where):
        route = []
        for w in range(wide):
            for n in range(narrow):
                to = where(n // CORES, n % CORES)
                if to is not None:
                    ahead, chip, unit = to
                    target = (w + ahead) % wide * narrow + chip % chips * CORES + unit % CORES
                    route.append((w * narrow + n, target))
        return lax.ppermute(x, BOTH, route)

    def swap(x):
        return permute(x, lambda y, u: (0, y, u + 1))

    turns = range(chips)
    thirds = [[t for t in turns if t % CORES == u] for u in range(CORES)]
    plan = [
        [("b", t) for t in turns] + [("c", t) for t in thirds[0]],
        [("c", t) for t in thirds[1]] + [("b", t) for t in turns],
    ]
    length = max(map(len, plan))
    plan = [p + [None] * (length - len(p)) for p in plan]

    def onward(total):
        part = {"b": total[:half], "c": total[half:]}
        ahead = {"b": SECOND_STRIDE, "c": THIRD_STRIDE}
        got = []
        for pair in zip(*plan, strict=True):
            kinds = [p and p[0] for p in pair]

            def where(y, u, pair=pair):
                return pair[u] and (ahead[pair[u][0]], y + pair[u][1], u)

            if kinds[0] == kinds[1] or None in kinds:
                message = part[kinds[0] or kinds[1]]
            else:
                message = jnp.where(lead, part[kinds[0]], part[kinds[1]])
            got.append(permute(message, where))
        return got

    def collect(got, kind):
        sums = []
        for u in range(CORES):
            terms = [x for x, pair in zip(got, zip(*plan)) if pair[u] and pair[u][0] == kind]
            sums.append(functools.reduce(jnp.add, terms) if terms else jnp.zeros_like(got[0]))
        return jnp.where(lead, sums[0], sums[1])

    tile_shape = jax.ShapeDtypeStruct((kb, ib, jb), tiles.dtype)
    block_a, block_b, block_c, share = f32(ib, rank), f32(jb, rank), f32(kb, rank), f32(half + kb, rank)

    grams = f32(rank, rank)

    def scratch(x):
        return pltpu.VMEM(x.shape, x.dtype)

    slots = pltpu.SMEM(slot.shape, slot.dtype)
    args = a, b, c, va, vb, vc
    tile, a, b, c, va, bc_gram, now, base, keep, send = pl.pallas_call(
        functools.partial(first_kernel, **mults),
        out_shape=(tile_shape, block_a, block_b, block_c, block_a, grams, block_c, block_c, share, share),
        in_specs=[SMEM] * 2 + [HBM] * 8,
        out_specs=(VMEM,) * 10,
        scratch_shapes=[scratch(x) for x in (block_b, block_c, block_b, block_c, block_b, f32(2, STEP, jb, rank))]
        + [slots, pltpu.SemaphoreType.DMA((4,)), pltpu.SemaphoreType.DMA((7,))],
        compiler_params=GRANT,
    )(*pos, order, far, *map(in_hbm, args))
    none = jnp.zeros((half, rank), jnp.float32)

    def with_base(keep, send, base):
        for_b, for_c = jnp.where(chip == 0, base, none), jnp.where(chip == 1, base, none)
        return (
            keep + jnp.concatenate([for_b, for_c], axis=0),
            send + jnp.concatenate([none, for_c], axis=0),
        )

    def forward(x):
        return permute(x, lambda y, u: ((SECOND_STRIDE, THIRD_STRIDE)[y], y, u) if y < 2 else None)

    for s in range(STRATA):
        keep, send = with_base(keep, send, base)
        received = swap(send)
        if s == 0:
            past = forward(now)
        total = keep + received
        if s > 0:
            bc_gram, terms = pl.pallas_call(
                functools.partial(terms_kernel, **mults),
                out_shape=(grams, share),
                in_specs=[VMEM] * 5,
                out_specs=(VMEM,) * 2,
                compiler_params=GRANT,
            )(*ours, mine, b, c)
            total = total - terms
        total, tile, a, va, b, c, bc_gram = lax.optimization_barrier((total, tile, a, va, b, c, bc_gram))
        if s + 1 == STRATA:
            break
        got = onward(total)
        tile, a, va, ata, z = pl.pallas_call(
            functools.partial(window_kernel, scale=scale_a, stratum=s + 1),
            out_shape=(tile_shape, block_a, block_a, grams, f32(kb, jb, rank)),
            in_specs=[HBM] * 2 + [VMEM] * 6,
            out_specs=(VMEM,) * 5,
            scratch_shapes=[slots, pltpu.SemaphoreType.DMA, pltpu.SemaphoreType.DMA],
            compiler_params=GRANT,
        )(order, far, tile, a, va, b, c, bc_gram)
        ata_other = swap(ata)
        got, a, va, z = lax.optimization_barrier((got, a, va, z))
        ours = ata, ata_other
        mine = jnp.concatenate([collect(got, "b"), collect(got, "c")], axis=0)
        other = swap(mine)
        before = past
        if s + 2 < STRATA:
            past = forward(jnp.where(chip == 0, mine[:half], mine[half:]))
        b, c, keep, send = pl.pallas_call(
            functools.partial(gradient_kernel, **mults),
            out_shape=(block_b, block_c, share, share),
            in_specs=[SMEM] + [VMEM] * 5,
            out_specs=(VMEM,) * 4,
            scratch_shapes=[scratch(x) for x in (block_b, block_c) + (f32(STEP, ib, rank),) * 2],
            compiler_params=GRANT,
        )(pos[0], tile, z, a, mine, other)
        base = (1.0 + momentum) * jnp.where(chip == 0, mine[:half], (1.0 / CORES) * c) - momentum * before
    beside = swap(total[:half])
    same = [permute(total, lambda y, u, t=t: (0, y + t, u)) for t in range(1, chips)]
    cross = [permute(total[:half], lambda y, u, t=t: (0, y + t, u + 1)) for t in range(1, chips)]
    a = pl.pallas_call(
        functools.partial(last_kernel, scale=scale_a),
        out_shape=f32(ib, rank),
        in_specs=[VMEM] * 6,
        out_specs=VMEM,
        compiler_params=GRANT,
    )(tile, a, va, b, c, bc_gram)
    beside, same, cross, a = lax.optimization_barrier((beside, same, cross, a))
    b, c = pl.pallas_call(
        final_kernel,
        out_shape=(block_b, block_c),
        in_specs=[SMEM] + [VMEM] * 4,
        out_specs=(VMEM,) * 2,
        compiler_params=GRANT,
    )(pos[0], total, beside, jnp.stack(same), jnp.stack(cross))
    return a, b, c


def solution(mesh):
    return program(mesh)


def program(mesh):
    return jax.shard_map(
        shards,
        mesh=mesh,
        in_specs=(
            P(None, None, BOTH, None),
            P(BOTH, None),
            P(BOTH, None),
            P("wide", None),
            P("wide", None),
            P(BOTH, None),
            P("wide", None),
            P("wide", None),
        ),
        out_specs=(P(BOTH, None), P("wide", None), P("wide", None)),
        check_vma=False,
    )
```
